512 devices in a mesh: section: 4 (over y_hi, core), fsdp: 32 (over y_lo, z), ep: 4 (over x).
Axes of the slice: x: 4, y: 4 (y_hi: 2, y_lo: 2; y = y_hi * 2 + y_lo), z: 16, core: 2. Of those that a mesh axis runs over, the one named last changes fastest.
Arguments:
- hidden: bfloat16 [32768, 7168], P(('section', 'fsdp'), 'ep'), may hold values from -6 to 6
- attn_gain: float32 [7168], replicated, may hold values from 0.25 to 1.75
- q_gain: float32 [1536], replicated, may hold values from 0.25 to 1.75
- kv_gain: float32 [512], replicated, may hold values from 0.25 to 1.75
- down_weight: bfloat16 [7168, 2112], P('fsdp', 'ep'), may hold values from -0.0625 to 0.0625
Outputs:
- q_latent: bfloat16 [32768, 1536], P(('section', 'fsdp', 'ep'))
- kv_cache: bfloat16 [32768, 576], P(('section', 'fsdp', 'ep'))
The draws below stay inside these ranges and needn't reach their ends.
All inputs are finite; a program needn't handle non-finite values.
Results may differ from the reference program's by a relative error of at most 0.0049.
Values may be sent and summed in bfloat16 or wider, within the bound.
A program may use at most 64 MiB of HBM per device.

```python
import jax
import jax.numpy as jnp
from jax import lax

D = 7168
QL = 1536
KVL = 512
ROPE = 64
TOK_DEV = 256
LENGTH = 4096
LAT = 2112
TOKENS = 32768
N_FSDP = 32


def block_levels(own_key, dims, split, low, largest):
    level, own = 1.0, jax.random.fold_in(own_key, 6)
    for dim, parts in split:
        heights = jnp.exp(jax.random.uniform(jax.random.fold_in(own, dim), (parts,), jnp.float32, low / len(split), largest / len(split)))
        level = level * jnp.repeat(heights, dims[dim] // parts).reshape([-1 if axis == dim else 1 for axis in range(len(dims))])
    return level


def bell_draw(own_key, shape, scale, reach, cuts=(), held_as=jnp.bfloat16):
    level = block_levels(own_key, shape, cuts, -0.22, 0.18) if cuts else 1.0
    values = jax.random.normal(own_key, shape, jnp.float32) * scale * level
    return jnp.minimum(jnp.maximum(values, -reach), reach).astype(held_as)


def setup_inputs(seed: int = 0) -> dict:
    splits = jax.random.split(jax.random.key(seed), 6)
    hidden = bell_draw(splits[0], (TOKENS, D), 1.0, 6.0, ((0, 128), (1, 4)))
    attn_gain = jnp.clip(1.0 + 0.15 * jax.random.normal(splits[1], (D,), jnp.float32), 0.25, 1.75)
    q_gain = jnp.clip(1.0 + 0.15 * jax.random.normal(splits[2], (QL,), jnp.float32), 0.25, 1.75)
    kv_gain = jnp.clip(1.0 + 0.15 * jax.random.normal(splits[3], (KVL,), jnp.float32), 0.25, 1.75)
    down_weight = bell_draw(splits[4], (D, LAT), D ** -0.5, 0.0625, ((0, 32), (1, 4)))
    return {"hidden": hidden, "attn_gain": attn_gain, "q_gain": q_gain, "kv_gain": kv_gain, "down_weight": down_weight}


epsilon = 1e-06
rope_base = 10000.0

def root_scale(values, gain):
    mean_square = lax.optimization_barrier(jnp.mean(values * values, axis=-1, keepdims=True))
    return values * lax.rsqrt(mean_square + epsilon) * gain

def rotate(latent, position):
    half_rope = ROPE // 2
    frequency = rope_base ** (-(jnp.arange(half_rope).astype(jnp.float32) / half_rope))
    angle = position.astype(jnp.float32)[:, None] * frequency[None, :]
    first = latent[:, QL + KVL:QL + KVL + half_rope]
    second = latent[:, QL + KVL + half_rope:]
    cosine = jnp.cos(angle)
    sine = jnp.sin(angle)
    return jnp.concatenate([first * cosine - second * sine, second * cosine + first * sine], axis=1)

def reference(hidden, attn_gain, q_gain, kv_gain, down_weight):
    section_rows = TOK_DEV * N_FSDP
    moved = jnp.roll(hidden, section_rows, axis=0)
    grouped = moved.reshape(TOKENS // TOK_DEV, TOK_DEV, D)

    def one_block(index_rows):
        index, rows = index_rows
        normed = root_scale(rows.astype(jnp.float32), attn_gain).astype(jnp.bfloat16)
        latent = jnp.dot(normed, down_weight, preferred_element_type=jnp.float32)
        query = root_scale(latent[:, :QL], q_gain).astype(jnp.bfloat16)
        key_value = root_scale(latent[:, QL:QL + KVL], kv_gain)
        row_index = index * TOK_DEV + jnp.arange(TOK_DEV).astype(jnp.int32)
        position = row_index % section_rows % LENGTH
        cache = jnp.concatenate([key_value, rotate(latent, position)], axis=1).astype(jnp.bfloat16)
        return (query, cache)
    indices = jnp.arange(TOKENS // TOK_DEV).astype(jnp.int32)
    query, cache = lax.map(one_block, (indices, grouped))
    return (query.reshape(TOKENS, QL), cache.reshape(TOKENS, KVL + ROPE))
```

```python
import functools

import jax
import jax.numpy as jnp
from jax import lax
from jax.experimental import pallas as pl
from jax.experimental.pallas import tpu as pltpu
from jax.sharding import PartitionSpec as P

MESH = pl.DeviceIdType.MESH

QL = 1536
KVL = 512
ROPE = 64
LENGTH = 4096
D = 7168

epsilon = 1e-06
rope_base = 10000.0

ROWS = 256
KS = 1792
WR = 224
WC = 528
PARTS = 2
PR = WR // PARTS
HALF = ROWS // 2
QUARTER = ROWS // 4
WIDE = 640
NZ = 16
HOPS = NZ // 2


def kernel(
    hid, w, gain, q_gain, kv_gain, cosine, sine, q_out, kv_out,
    xbuf, xg, wbuf, acc, ssq, lsend, lrecv,
    local_sem, xs, xr, zs, zr, ys, yr, cs, cr, ls, lr,
):
    sec = lax.axis_index("section")
    f = lax.axis_index("fsdp")
    x = lax.axis_index("ep")
    core = sec % 2
    yl = f // NZ
    z = f % NZ
    y = (sec // 2) * 2 + yl
    way = 1 - 2 * core

    def place(y_, z_, core_, x_):
        y_ = (y_ + 8) % 4
        z_ = (z_ + 2 * NZ) % NZ
        return ((y_ // 2) * 2 + core_, (y_ % 2) * NZ + z_, (x_ + 4) % 4)

    ahead_z = place(y, z + way, core, x)
    ahead_y = place(y + way, z, core, x)
    sibling = place(y, z, 1 - core, x)
    right = place(y, z, core, x + 1)
    left = place(y, z, core, x - 1)

    barrier = pltpu.get_barrier_semaphore()
    partners = [
        place(y, z + 1, core, x), place(y, z - 1, core, x),
        place(y + 1, z, core, x), place(y - 1, z, core, x),
        sibling, right, left,
    ]
    for other in range(4):
        partners.append(((sec + 1) % 4, f, other))
        partners.append(((sec + 3) % 4, f, other))
    for partner in partners:
        pl.semaphore_signal(barrier, inc=1, device_id=partner, device_id_type=MESH)
    pl.semaphore_wait(barrier, len(partners))

    def rdma(src, dst, send, recv, device):
        return pltpu.make_async_remote_copy(
            src_ref=src, dst_ref=dst, send_sem=send, recv_sem=recv,
            device_id=device, device_id_type=MESH,
        )

    sends = []

    def start(copy):
        copy.start()
        sends.append(copy)

    def x_rows(owner, half):
        return xbuf.at[owner, pl.ds(half * HALF, HALF)]

    def x_own(half, index, device):
        return rdma(hid.at[pl.ds(half * HALF, HALF)], x_rows(x, half), xs.at[index], xr.at[index], device)

    x_left, x_right, x_far = (x + 3) % 4, (x + 1) % 4, (x + 2) % 4

    def w_rows(slot, part):
        return wbuf.at[pl.ds(pl.multiple_of(slot * WR + part * PR, PR), PR)]

    def ring_slot(d):
        return yl * NZ + (z - way * d + NZ) % NZ

    def pair_slot(j):
        return (1 - yl) * NZ + (z - way * (j + 1 - core) + NZ) % NZ

    def cross_ring_slot(d):
        return yl * NZ + (z + way * d + NZ) % NZ

    def cross_pair_slot(j):
        return (1 - yl) * NZ + (z + way * (j + core) + NZ) % NZ

    def w_src(d, part):
        if d == 0:
            return w.at[pl.ds(part * PR, PR)]
        return w_rows(ring_slot(d), part)

    own_x = pltpu.make_async_copy(hid, xbuf.at[x], local_sem.at[0])
    own_w = pltpu.make_async_copy(w, wbuf.at[pl.ds(pl.multiple_of(f * WR, WR), WR)], local_sem.at[1])

    def z_copy(d, part):
        i = d * PARTS + part
        return rdma(w_src(d, part), w_rows(ring_slot(d), part), zs.at[i], zr.at[i], ahead_z)

    def y_copy(d, part):
        i = (d - 1 + core) * PARTS + part
        return rdma(w_src(d, part), w_rows(ring_slot(d), part), ys.at[i], yr.at[i], ahead_y)

    def cross_ring(d, part):
        i = (d - 1) * PARTS + part
        rows = w_rows(ring_slot(d), part)
        return rdma(rows, rows, cs.at[i], cr.at[i], sibling)

    def cross_pair(j, part):
        i = (HOPS - 1 + j) * PARTS + part
        rows = w_rows(pair_slot(j), part)
        return rdma(rows, rows, cs.at[i], cr.at[i], sibling)

    def hand_on_pair(j):
        for part in range(PARTS):
            i = j * PARTS + part
            rows = w_rows(pair_slot(j), part)
            rdma(rows, rows, ys.at[i], yr.at[i], ahead_y).wait_recv()
            start(cross_pair(j, part))

    def prepare(owner, half):
        g = gain[owner]

        def block(i, carry):
            rows = pl.ds(pl.multiple_of(half * HALF + i * 16, 16), 16)
            v = xbuf[owner, rows, :].astype(jnp.float32)
            xg[owner, rows, :] = (v * g).astype(jnp.bfloat16)
            total = ssq[rows, :]
            for t in range(KS // 128):
                piece = v[:, t * 128 : (t + 1) * 128]
                total = total + piece * piece
            ssq[rows, :] = total
            return carry

        lax.fori_loop(0, HALF // 16, block, 0)

    def multiply(owner):
        columns = wbuf[pl.ds(pl.multiple_of(owner * KS, KS), KS), :]
        for half in range(2):
            rows = pl.ds(half * HALF, HALF)
            acc[rows, :WC] += jnp.dot(xg[owner, rows, :], columns, preferred_element_type=jnp.float32)

    for part in range(PARTS):
        start(z_copy(0, part))

        @pl.when(core == 1)
        def _():
            y_copy(0, part).start()

    start(x_own(0, 0, right))
    start(x_own(1, 1, left))
    start(x_own(1, 2, right))
    start(x_own(0, 3, left))
    own_x.start()
    own_w.start()
    ssq[...] = jnp.zeros_like(ssq)
    acc[...] = jnp.zeros_like(acc)
    own_x.wait()
    prepare(x, 0)
    prepare(x, 1)
    own_w.wait()

    for d in range(1, HOPS + 1):
        for part in range(PARTS):
            z_copy(d - 1, part).wait_recv()
            if d < HOPS:
                start(z_copy(d, part))
                y_copy(d, part).start()
                start(cross_ring(d, part))
            else:

                @pl.when(core == 0)
                def _():
                    y_copy(d, part).start()

        if d >= 3:
            hand_on_pair(d - 3)
        if d == HOPS - 2:
            x_own(0, 0, right).wait_recv()
            start(rdma(x_rows(x_left, 0), x_rows(x_left, 0), xs.at[4], xr.at[4], right))
            x_own(1, 1, left).wait_recv()
            start(rdma(x_rows(x_right, 1), x_rows(x_right, 1), xs.at[5], xr.at[5], left))
            prepare(x_left, 0)
            prepare(x_right, 1)
    hand_on_pair(HOPS - 2)
    hand_on_pair(HOPS - 1)

    x_own(1, 2, right).wait_recv()
    prepare(x_left, 1)
    x_own(0, 3, left).wait_recv()
    prepare(x_right, 0)

    for i in range((2 * HOPS - 1) * PARTS):
        rows = w_rows(0, 0)
        rdma(rows, rows, cs.at[i], cr.at[i], sibling).wait_recv()

    def slice_step(i, carry):
        multiply(lax.rem(x_left + i, 4))
        return carry

    lax.fori_loop(0, 3, slice_step, 0)

    for half in range(2):
        rows = x_rows(x_far, half)
        rdma(rows, rows, xs.at[4 + half], xr.at[4 + half], right).wait_recv()
        prepare(x_far, half)
    multiply(x_far)

    scale = lax.rsqrt(jnp.sum(ssq[...], axis=1, keepdims=True) / D + epsilon)
    out = pltpu.roll(acc[...] * scale, x * 16, 1).astype(jnp.bfloat16)
    for other in range(4):
        lsend[other] = out[other * QUARTER : (other + 1) * QUARTER]
    for other in range(4):
        start(rdma(lsend.at[other], lrecv.at[x], ls.at[other], lr.at[x], ((sec + 1) % 4, f, other)))
    for other in range(4):
        rdma(lsend.at[other], lrecv.at[other], ls.at[other], lr.at[other], ((sec + 1) % 4, f, other)).wait_recv()

    pieces = [lrecv[other].astype(jnp.float32) for other in range(4)]
    tiles = []
    for other in range(4):
        first = pieces[other][:, :128]
        if other:
            first = first + pieces[other - 1][:, 512:]
        tiles.append(first)
        tiles.append(pieces[other][:, 128:512])
    latent = jnp.concatenate(tiles, axis=1)
    rope = pieces[3][:, 512:]

    q = latent[:, :QL]
    q_out[...] = (
        q * lax.rsqrt(jnp.mean(q * q, axis=1, keepdims=True) + epsilon) * q_gain[...]
    ).astype(jnp.bfloat16)
    k = latent[:, QL:]
    kv_out[:, :KVL] = (
        k * lax.rsqrt(jnp.mean(k * k, axis=1, keepdims=True) + epsilon) * kv_gain[...]
    ).astype(jnp.bfloat16)
    lane = lax.broadcasted_iota(jnp.int32, rope.shape, 1)
    swapped = jnp.where(lane < ROPE // 2, pltpu.roll(rope, 128 - ROPE // 2, 1), pltpu.roll(rope, ROPE // 2, 1))
    turned = rope * cosine[...] + swapped * sine[...]
    kv_out[:, KVL:] = turned[:, :ROPE].astype(jnp.bfloat16)

    for copy in sends:
        copy.wait_send()
    for i in range(HOPS * PARTS):
        rows = w_rows(0, 0)
        rdma(rows, rows, ys.at[i], yr.at[i], ahead_y).wait_send()


def on_device(hidden, attn_gain, q_gain, kv_gain, down_weight):
    quarter = QUARTER
    half_rope = ROPE // 2
    row_index = lax.axis_index("fsdp") * ROWS + lax.axis_index("ep") * quarter + jnp.arange(quarter)
    position = row_index % LENGTH
    frequency = rope_base ** (-(jnp.arange(half_rope).astype(jnp.float32) / half_rope))
    angle = position.astype(jnp.float32)[:, None] * frequency[None, :]
    cosine, sine = jnp.cos(angle), jnp.sin(angle)
    rest = jnp.zeros((quarter, 128 - ROPE), jnp.float32)
    cosine = jnp.concatenate([cosine, cosine, rest], axis=1)
    sine = jnp.concatenate([-sine, sine, rest], axis=1)

    vmem = pl.BlockSpec(memory_space=pltpu.VMEM)
    hbm = pl.BlockSpec(memory_space=pl.ANY)
    dma = pltpu.SemaphoreType.DMA
    return pl.pallas_call(
        kernel,
        out_shape=(
            jax.ShapeDtypeStruct((quarter, QL), jnp.bfloat16),
            jax.ShapeDtypeStruct((quarter, KVL + ROPE), jnp.bfloat16),
        ),
        in_specs=[hbm, hbm, vmem, vmem, vmem, vmem, vmem],
        out_specs=(vmem, vmem),
        scratch_shapes=[
            pltpu.VMEM((4, ROWS, KS), jnp.bfloat16),
            pltpu.VMEM((4, ROWS, KS), jnp.bfloat16),
            pltpu.VMEM((D, WC), jnp.bfloat16),
            pltpu.VMEM((ROWS, WIDE), jnp.float32),
            pltpu.VMEM((ROWS, 128), jnp.float32),
            pltpu.VMEM((4, QUARTER, WIDE), jnp.bfloat16),
            pltpu.VMEM((4, QUARTER, WIDE), jnp.bfloat16),
            dma((2,)),
            dma((6,)), dma((6,)),
            dma((HOPS * PARTS,)), dma((HOPS * PARTS,)),
            dma((HOPS * PARTS,)), dma((HOPS * PARTS,)),
            dma(((2 * HOPS - 1) * PARTS,)), dma(((2 * HOPS - 1) * PARTS,)),
            dma((4,)), dma((4,)),
        ],
        compiler_params=pltpu.CompilerParams(collective_id=0, has_side_effects=True, vmem_limit_bytes=50 * 2**20),
    )(
        hidden, down_weight, attn_gain.reshape(4, 1, KS), q_gain.reshape(1, QL), kv_gain.reshape(1, KVL), cosine, sine,
    )


def solution(mesh):
    placed = (P(("section", "fsdp"), "ep"), P(), P(), P(), P("fsdp", "ep"))
    return jax.shard_map(
        on_device,
        mesh=mesh,
        in_specs=placed,
        out_specs=(P(("section", "fsdp", "ep"), None), P(("section", "fsdp", "ep"), None)),
        check_vma=False,
    )
```

```python
import functools

import jax
import jax.numpy as jnp
from jax import lax
from jax.experimental import pallas as pl
from jax.experimental.pallas import tpu as pltpu
from jax.sharding import PartitionSpec as P

MESH = pl.DeviceIdType.MESH

QL = 1536
KVL = 512
ROPE = 64
LENGTH = 4096
D = 7168

epsilon = 1e-06
rope_base = 10000.0

ROWS = 256
KS = 1792
WR = 224
WC = 528
PARTS = 7
PR = WR // PARTS
HALF = ROWS // 2
QUARTER = ROWS // 4
WIDE = 640
NZ = 16
HOPS = NZ // 2


def kernel(
    hid, w, gain, q_gain, kv_gain, q_out, kv_out,
    xbuf, xg, wbuf, acc, ssq, lsend, lrecv, gain_v, q_gain_v, kv_gain_v, cosine, sine,
    local_sem, xs, xr, zs, zr, ys, yr, cs, cr, ls, lr, rounds,
):
    sec = lax.axis_index("section")
    f = lax.axis_index("fsdp")
    x = lax.axis_index("ep")
    core = sec % 2
    yl = f // NZ
    z = f % NZ
    y = (sec // 2) * 2 + yl
    way = 1 - 2 * core

    def place(y_, z_, core_, x_):
        y_ = (y_ + 8) % 4
        z_ = (z_ + 2 * NZ) % NZ
        return ((y_ // 2) * 2 + core_, (y_ % 2) * NZ + z_, (x_ + 4) % 4)

    ahead_z = place(y, z + way, core, x)
    ahead_y = place(y + way, z, core, x)
    sibling = place(y, z, 1 - core, x)
    right = place(y, z, core, x + 1)
    left = place(y, z, core, x - 1)

    barrier = pltpu.get_barrier_semaphore()
    up_y, down_y = place(y + 1, z, core, x), place(y - 1, z, core, x)
    partners = [place(y, z + 1, core, x), place(y, z - 1, core, x), up_y, down_y, sibling, right, left]

    def tell(semaphore, devices):
        for device in devices:
            pl.semaphore_signal(semaphore, inc=1, device_id=device, device_id_type=MESH)

    tell(barrier, partners)
    pl.semaphore_wait(barrier, len(partners))

    tell(rounds.at[0], (right, left))

    def next_round(n):
        if n < 3:
            pl.semaphore_wait(rounds.at[n], 2)
            tell(rounds.at[n + 1], (up_y, down_y) if n < 2 else (sibling,))
        else:
            pl.semaphore_wait(rounds.at[n], 1)

    def rdma(src, dst, send, recv, device):
        return pltpu.make_async_remote_copy(
            src_ref=src, dst_ref=dst, send_sem=send, recv_sem=recv,
            device_id=device, device_id_type=MESH,
        )

    sends = []

    def start(copy):
        copy.start()
        sends.append(copy)

    def x_rows(owner, half):
        return xbuf.at[owner, pl.ds(half * HALF, HALF)]

    def x_own(half, index, device):
        return rdma(hid.at[pl.ds(half * HALF, HALF)], x_rows(x, half), xs.at[index], xr.at[index], device)

    x_left, x_right, x_far = (x + 3) % 4, (x + 1) % 4, (x + 2) % 4

    def w_rows(slot, part):
        return wbuf.at[pl.ds(pl.multiple_of(slot * WR + part * PR, PR), PR)]

    def ring_slot(d):
        return yl * NZ + (z - way * d + NZ) % NZ

    def pair_slot(j):
        return (1 - yl) * NZ + (z - way * (j + 1 - core) + NZ) % NZ

    def cross_ring_slot(d):
        return yl * NZ + (z + way * d + NZ) % NZ

    def cross_pair_slot(j):
        return (1 - yl) * NZ + (z + way * (j + core) + NZ) % NZ

    def w_src(d, part):
        if d == 0:
            return w.at[pl.ds(part * PR, PR)]
        return w_rows(ring_slot(d), part)

    own_x = pltpu.make_async_copy(hid, xbuf.at[x], local_sem.at[0])
    own_gains = [
        pltpu.make_async_copy(gain, gain_v, local_sem.at[2]),
        pltpu.make_async_copy(q_gain, q_gain_v, local_sem.at[3]),
        pltpu.make_async_copy(kv_gain, kv_gain_v, local_sem.at[4]),
    ]
    own_w = pltpu.make_async_copy(w, wbuf.at[pl.ds(pl.multiple_of(f * WR, WR), WR)], local_sem.at[1])

    def z_copy(d, part):
        i = d * PARTS + part
        return rdma(w_src(d, part), w_rows(ring_slot(d), part), zs.at[i], zr.at[i], ahead_z)

    def y_copy(d, part):
        i = (d - 1 + core) * PARTS + part
        return rdma(w_src(d, part), w_rows(ring_slot(d), part), ys.at[i], yr.at[i], ahead_y)

    def diagonal(part):
        i = (HOPS - 1) * PARTS + part
        rows = w_rows(ring_slot(HOPS - 1), part)
        return rdma(rows, rows, ys.at[i], yr.at[i], place(y + way, z + way, core, x))

    def shard(slot):
        return wbuf.at[pl.ds(pl.multiple_of(slot * WR, WR), WR)]

    def cross(slot, i):
        return rdma(shard(slot), shard(slot), cs.at[i], cr.at[i], sibling)

    def each_part(step):
        def body(part, carry):
            step(part)
            return carry

        lax.fori_loop(0, PARTS, body, 0)

    def hand_on_pair(j):
        def step(part):
            i = j * PARTS + part
            rows = w_rows(pair_slot(j), part)
            rdma(rows, rows, ys.at[i], yr.at[i], ahead_y).wait_recv()

        each_part(step)
        start(cross(pair_slot(j), HOPS - 1 + j))

    def angles():
        half_rope = ROPE // 2
        shape = (QUARTER, 128)
        lane = lax.broadcasted_iota(jnp.int32, shape, 1)
        row = lax.broadcasted_iota(jnp.int32, shape, 0) + f * ROWS + x * QUARTER
        power = (lane % half_rope).astype(jnp.float32) / half_rope
        angle = (row % LENGTH).astype(jnp.float32) * (rope_base ** (-power))
        cosine[...] = jnp.cos(angle)
        sine[...] = jnp.where(lane < half_rope, -jnp.sin(angle), jnp.sin(angle))

    def prepare(owner, half):
        g = gain_v[pl.ds(pl.multiple_of(owner * KS, KS), KS)][None, :]

        def block(i, carry):
            rows = pl.ds(pl.multiple_of(half * HALF + i * 16, 16), 16)
            v = xbuf[owner, rows, :].astype(jnp.float32)
            xg[owner, rows, :] = (v * g).astype(jnp.bfloat16)
            total = ssq[rows, :]
            for t in range(KS // 128):
                piece = v[:, t * 128 : (t + 1) * 128]
                total = total + piece * piece
            ssq[rows, :] = total
            return carry

        lax.fori_loop(0, HALF // 16, block, 0)

    def multiply(owner):
        columns = wbuf[pl.ds(pl.multiple_of(owner * KS, KS), KS), :]
        for half in range(2):
            rows = pl.ds(half * HALF, HALF)
            acc[rows, :WC] += jnp.dot(xg[owner, rows, :], columns, preferred_element_type=jnp.float32)

    def first(part):
        z_copy(0, part).start()

        @pl.when(core == 1)
        def _():
            y_copy(0, part).start()

    each_part(first)
    start(x_own(0, 0, right))
    start(x_own(1, 1, left))
    start(x_own(1, 2, right))
    start(x_own(0, 3, left))
    own_x.start()
    own_w.start()
    for copy in own_gains:
        copy.start()
    angles()
    ssq[...] = jnp.zeros_like(ssq)
    acc[...] = jnp.zeros_like(acc)
    own_x.wait()
    for copy in own_gains:
        copy.wait()
    prepare(x, 0)
    prepare(x, 1)
    own_w.wait()

    for d in range(1, HOPS + 1):

        def step(part):
            z_copy(d - 1, part).wait_recv()
            if d < HOPS:
                z_copy(d, part).start()
                if d == HOPS - 1:

                    @pl.when(core == 0)
                    def _():
                        diagonal(part).start()

                y_copy(d, part).start()

        each_part(step)
        if d < HOPS:
            start(cross(ring_slot(d), d - 1))
        if d >= 3:
            hand_on_pair(d - 3)
        if d <= 4:
            next_round(d - 1)
        if d == 5:
            x_own(0, 0, right).wait_recv()
            start(rdma(x_rows(x_left, 0), x_rows(x_left, 0), xs.at[4], xr.at[4], right))
            x_own(1, 1, left).wait_recv()
            start(rdma(x_rows(x_right, 1), x_rows(x_right, 1), xs.at[5], xr.at[5], left))
        if d == 6:
            prepare(x_left, 0)
        if d == 7:
            prepare(x_right, 1)
    hand_on_pair(HOPS - 2)
    hand_on_pair(HOPS - 1)

    x_own(1, 2, right).wait_recv()
    prepare(x_left, 1)
    x_own(0, 3, left).wait_recv()
    prepare(x_right, 0)

    for i in range(2 * HOPS - 1):
        cross(0, i).wait_recv()

    def slice_step(i, carry):
        multiply(lax.rem(x_left + i, 4))
        return carry

    lax.fori_loop(0, 3, slice_step, 0)

    for half in range(2):
        rows = x_rows(x_far, half)
        rdma(rows, rows, xs.at[4 + half], xr.at[4 + half], right).wait_recv()
        prepare(x_far, half)
    multiply(x_far)

    scale = lax.rsqrt(jnp.sum(ssq[...], axis=1, keepdims=True) / D + epsilon)
    out = pltpu.roll(acc[...] * scale, x * 16, 1).astype(jnp.bfloat16)
    for other in range(4):
        lsend[other] = out[other * QUARTER : (other + 1) * QUARTER]
    for other in range(4):
        start(rdma(lsend.at[other], lrecv.at[x], ls.at[other], lr.at[x], ((sec + 1) % 4, f, other)))
    for other in range(4):
        rdma(lsend.at[other], lrecv.at[other], ls.at[other], lr.at[other], ((sec + 1) % 4, f, other)).wait_recv()

    pieces = [lrecv[other].astype(jnp.float32) for other in range(4)]
    tiles = []
    for other in range(4):
        first = pieces[other][:, :128]
        if other:
            first = first + pieces[other - 1][:, 512:]
        tiles.append(first)
        tiles.append(pieces[other][:, 128:512])
    latent = jnp.concatenate(tiles, axis=1)
    rope = pieces[3][:, 512:]

    q = latent[:, :QL]
    q_out[...] = (
        q * lax.rsqrt(jnp.mean(q * q, axis=1, keepdims=True) + epsilon) * q_gain_v[...][None, :]
    ).astype(jnp.bfloat16)
    k = latent[:, QL:]
    kv_out[:, :KVL] = (
        k * lax.rsqrt(jnp.mean(k * k, axis=1, keepdims=True) + epsilon) * kv_gain_v[...][None, :]
    ).astype(jnp.bfloat16)
    lane = lax.broadcasted_iota(jnp.int32, rope.shape, 1)
    swapped = jnp.where(lane < ROPE // 2, pltpu.roll(rope, 128 - ROPE // 2, 1), pltpu.roll(rope, ROPE // 2, 1))
    turned = rope * cosine[...] + swapped * sine[...]
    kv_out[:, KVL:] = turned[:, :ROPE].astype(jnp.bfloat16)

    for copy in sends:
        copy.wait_send()
    def sent(i, carry):
        rows = w_rows(0, 0)
        rdma(rows, rows, zs.at[i], zr.at[i], ahead_z).wait_send()
        rdma(rows, rows, ys.at[i], yr.at[i], ahead_y).wait_send()
        return carry

    lax.fori_loop(0, HOPS * PARTS, sent, 0)


def on_device(hidden, attn_gain, q_gain, kv_gain, down_weight):
    quarter = QUARTER
    vmem = pl.BlockSpec(memory_space=pltpu.VMEM)
    free = pl.BlockSpec(memory_space=pl.ANY)
    hbm = pl.BlockSpec(memory_space=pltpu.HBM)
    dma = pltpu.SemaphoreType.DMA
    return pl.pallas_call(
        kernel,
        out_shape=(
            jax.ShapeDtypeStruct((quarter, QL), jnp.bfloat16),
            jax.ShapeDtypeStruct((quarter, KVL + ROPE), jnp.bfloat16),
        ),
        in_specs=[hbm, free, hbm, hbm, hbm],
        out_specs=(vmem, vmem),
        scratch_shapes=[
            pltpu.VMEM((4, ROWS, KS), jnp.bfloat16),
            pltpu.VMEM((4, ROWS, KS), jnp.bfloat16),
            pltpu.VMEM((D, WC), jnp.bfloat16),
            pltpu.VMEM((ROWS, WIDE), jnp.float32),
            pltpu.VMEM((ROWS, 128), jnp.float32),
            pltpu.VMEM((4, QUARTER, WIDE), jnp.bfloat16),
            pltpu.VMEM((4, QUARTER, WIDE), jnp.bfloat16),
            pltpu.VMEM((D,), jnp.float32),
            pltpu.VMEM((QL,), jnp.float32),
            pltpu.VMEM((KVL,), jnp.float32),
            pltpu.VMEM((QUARTER, 128), jnp.float32),
            pltpu.VMEM((QUARTER, 128), jnp.float32),
            dma((5,)),
            dma((6,)), dma((6,)),
            dma((HOPS * PARTS,)), dma((HOPS * PARTS,)),
            dma((HOPS * PARTS,)), dma((HOPS * PARTS,)),
            dma((2 * HOPS - 1,)), dma((2 * HOPS - 1,)),
            dma((4,)), dma((4,)),
            pltpu.SemaphoreType.REGULAR((4,)),
        ],
        compiler_params=pltpu.CompilerParams(collective_id=0, has_side_effects=True, vmem_limit_bytes=56_000_000),
    )(
        hidden, down_weight, attn_gain, q_gain, kv_gain,
    )


def solution(mesh):
    placed = (P(("section", "fsdp"), "ep"), P(), P(), P(), P("fsdp", "ep"))
    return jax.shard_map(
        on_device,
        mesh=mesh,
        in_specs=placed,
        out_specs=(P(("section", "fsdp", "ep"), None), P(("section", "fsdp", "ep"), None)),
        check_vma=False,
    )
```

```python
import functools

import jax
import jax.numpy as jnp
from jax import lax
from jax.experimental import pallas as pl
from jax.experimental.pallas import tpu as pltpu
from jax.sharding import PartitionSpec as P

MESH = pl.DeviceIdType.MESH

QL = 1536
KVL = 512
ROPE = 64
LENGTH = 4096
D = 7168

epsilon = 1e-06
rope_base = 10000.0

ROWS = 256
KS = 1792
WR = 224
WC = 528
PARTS = 7
PR = WR // PARTS
GROUP = 4 * WR
HALF = ROWS // 2
QUARTER = ROWS // 4
WIDE = 640
NZ = 16
HOPS = NZ // 2


def kernel(
    hid, w, gain, q_gain, kv_gain, q_out, kv_out,
    xbuf, xg, wbuf, acc, ssq, lsend, lrecv, gain_v, q_gain_v, kv_gain_v, cosine, sine,
    local_sem, xs, xr, zs, zr, ys, yr, cs, cr, ls, lr, rounds,
):
    sec = lax.axis_index("section")
    f = lax.axis_index("fsdp")
    x = lax.axis_index("ep")
    core = sec % 2
    yl = f // NZ
    z = f % NZ
    y = (sec // 2) * 2 + yl
    way = 1 - 2 * core

    def place(y_, z_, core_, x_):
        y_ = (y_ + 8) % 4
        z_ = (z_ + 2 * NZ) % NZ
        return ((y_ // 2) * 2 + core_, (y_ % 2) * NZ + z_, (x_ + 4) % 4)

    ahead_z = place(y, z + way, core, x)
    ahead_y = place(y + way, z, core, x)
    sibling = place(y, z, 1 - core, x)
    right = place(y, z, core, x + 1)
    left = place(y, z, core, x - 1)

    barrier = pltpu.get_barrier_semaphore()
    up_y, down_y = place(y + 1, z, core, x), place(y - 1, z, core, x)
    partners = [place(y, z + 1, core, x), place(y, z - 1, core, x), up_y, down_y, sibling, right, left]

    def tell(semaphore, devices):
        for device in devices:
            pl.semaphore_signal(semaphore, inc=1, device_id=device, device_id_type=MESH)

    tell(barrier, partners)
    pl.semaphore_wait(barrier, len(partners))

    tell(rounds.at[0], (right, left))

    def next_round(n):
        if n < 3:
            pl.semaphore_wait(rounds.at[n], 2)
            tell(rounds.at[n + 1], (up_y, down_y) if n < 2 else (sibling,))
        else:
            pl.semaphore_wait(rounds.at[n], 1)

    def rdma(src, dst, send, recv, device):
        return pltpu.make_async_remote_copy(
            src_ref=src, dst_ref=dst, send_sem=send, recv_sem=recv,
            device_id=device, device_id_type=MESH,
        )

    sends = []

    def start(copy):
        copy.start()
        sends.append(copy)

    def x_rows(owner, half):
        return xbuf.at[owner, pl.ds(half * HALF, HALF)]

    def x_own(half, index, device):
        return rdma(hid.at[pl.ds(half * HALF, HALF)], x_rows(x, half), xs.at[index], xr.at[index], device)

    x_left, x_right, x_far = (x + 3) % 4, (x + 1) % 4, (x + 2) % 4

    def w_rows(slot, part):
        return wbuf.at[pl.ds(pl.multiple_of(slot * WR + part * PR, PR), PR)]

    def ring_slot(d):
        return yl * NZ + (z - way * d + NZ) % NZ

    def pair_slot(d):
        return (1 - yl) * NZ + (z - way * d + NZ) % NZ

    def w_src(d, part):
        if d == 0:
            return w.at[pl.ds(part * PR, PR)]
        return w_rows(ring_slot(d), part)

    own_x = pltpu.make_async_copy(hid, xbuf.at[x], local_sem.at[0])
    own_gains = [
        pltpu.make_async_copy(gain, gain_v, local_sem.at[2]),
        pltpu.make_async_copy(q_gain, q_gain_v, local_sem.at[3]),
        pltpu.make_async_copy(kv_gain, kv_gain_v, local_sem.at[4]),
    ]
    own_w = pltpu.make_async_copy(w, wbuf.at[pl.ds(pl.multiple_of(f * WR, WR), WR)], local_sem.at[1])

    def z_copy(d, part):
        i = d * PARTS + part
        return rdma(w_src(d, part), w_rows(ring_slot(d), part), zs.at[i], zr.at[i], ahead_z)

    def y_copy(d, part):
        i = d * PARTS + part
        return rdma(w_src(d, part), w_rows(ring_slot(d), part), ys.at[i], yr.at[i], ahead_y)

    def shard(slot):
        return wbuf.at[pl.ds(pl.multiple_of(slot * WR, WR), WR)]

    def cross(slot, i):
        return rdma(shard(slot), shard(slot), cs.at[i], cr.at[i], sibling)

    def each_part(step):
        def body(part, carry):
            step(part)
            return carry

        lax.fori_loop(0, PARTS, body, 0)

    def await_pair(d):
        def step(part):
            i = d * PARTS + part
            rows = w_rows(0, 0)
            rdma(rows, rows, ys.at[i], yr.at[i], ahead_y).wait_recv()

        each_part(step)

    def hand_on_pair(d):
        await_pair(d)
        cross(pair_slot(d), HOPS - 1 + d).start()

    def angles():
        half_rope = ROPE // 2
        shape = (QUARTER, 128)
        lane = lax.broadcasted_iota(jnp.int32, shape, 1)
        row = lax.broadcasted_iota(jnp.int32, shape, 0) + f * ROWS + x * QUARTER
        power = (lane % half_rope).astype(jnp.float32) / half_rope
        angle = (row % LENGTH).astype(jnp.float32) * (rope_base ** (-power))
        cosine[...] = jnp.cos(angle)
        sine[...] = jnp.where(lane < half_rope, -jnp.sin(angle), jnp.sin(angle))

    def prepare(owner, half):
        g = gain_v[pl.ds(pl.multiple_of(owner * KS, KS), KS)][None, :]

        def block(i, carry):
            rows = pl.ds(pl.multiple_of(half * HALF + i * 16, 16), 16)
            v = xbuf[owner, rows, :].astype(jnp.float32)
            xg[owner, rows, :] = (v * g).astype(jnp.bfloat16)
            total = ssq[rows, :]
            for t in range(KS // 128):
                piece = v[:, t * 128 : (t + 1) * 128]
                total = total + piece * piece
            ssq[rows, :] = total
            return carry

        lax.fori_loop(0, HALF // 16, block, 0)

    def multiply(parity, z_from):
        group = parity * (NZ // 4) + z_from % NZ // 4
        owner = group // 2
        depth = pl.ds(pl.multiple_of(group % 2 * GROUP, GROUP), GROUP)
        columns = wbuf[pl.ds(pl.multiple_of(group * GROUP, GROUP), GROUP), :]
        for half in range(2):
            rows = pl.ds(half * HALF, HALF)
            acc[rows, :WC] += jnp.dot(xg[owner, rows, depth], columns, preferred_element_type=jnp.float32)

    def multiply_all(parity, first_step, last_step):
        def body(i, carry):
            multiply(parity, z + 4 * i)
            return carry

        lax.fori_loop(first_step, last_step + 1, body, 0)

    def await_cross(first_index, last_index):
        for i in range(first_index, last_index + 1):
            cross(0, i).wait_recv()

    def first(part):
        z_copy(0, part).start()

        @pl.when(core == 1)
        def _():
            y_copy(0, part).start()

    each_part(first)
    start(x_own(0, 0, right))
    start(x_own(1, 1, left))
    start(x_own(1, 2, right))
    start(x_own(0, 3, left))
    own_x.start()
    own_w.start()
    for copy in own_gains:
        copy.start()
    angles()
    ssq[...] = jnp.zeros_like(ssq)
    acc[...] = jnp.zeros_like(acc)
    own_x.wait()
    for copy in own_gains:
        copy.wait()
    prepare(x, 0)
    prepare(x, 1)
    own_w.wait()

    for d in range(1, HOPS + 1):

        def step(part):
            z_copy(d - 1, part).wait_recv()
            if d < HOPS:
                z_copy(d, part).start()
            y_copy(d, part).start()

        each_part(step)
        if d < HOPS:
            start(cross(ring_slot(d), d - 1))
        if d == 2:

            @pl.when(core == 1)
            def _():
                hand_on_pair(0)

        if d >= 3:
            hand_on_pair(d - 2)
        if d <= 4:
            next_round(d - 1)
        if d == 5:
            x_own(0, 0, right).wait_recv()
            start(rdma(x_rows(x_left, 0), x_rows(x_left, 0), xs.at[4], xr.at[4], right))
            x_own(1, 1, left).wait_recv()
            start(rdma(x_rows(x_right, 1), x_rows(x_right, 1), xs.at[5], xr.at[5], left))
        if d == 6:
            prepare(x_left, 0)
            prepare(x_right, 1)
        if d == 7:
            x_own(1, 2, right).wait_recv()
            prepare(x_left, 1)
            x_own(0, 3, left).wait_recv()
            prepare(x_right, 0)
    hand_on_pair(HOPS - 1)
    for half in range(2):
        rows = x_rows(x_far, half)
        rdma(rows, rows, xs.at[4 + half], xr.at[4 + half], right).wait_recv()
        prepare(x_far, half)
    await_cross(0, HOPS - 2)
    multiply_all(yl, 0, 3)

    @pl.when(core == 0)
    def _():
        await_cross(HOPS - 1, HOPS - 1)

    await_cross(HOPS, 2 * HOPS - 2)
    multiply_all(1 - yl, 3, 5)
    await_pair(HOPS)
    multiply_all(1 - yl, 6, 6)

    scale = lax.rsqrt(jnp.sum(ssq[...], axis=1, keepdims=True) / D + epsilon)
    out = pltpu.roll(acc[...] * scale, x * 16, 1).astype(jnp.bfloat16)
    for other in range(4):
        lsend[other] = out[other * QUARTER : (other + 1) * QUARTER]
    for other in range(4):
        start(rdma(lsend.at[other], lrecv.at[x], ls.at[other], lr.at[x], ((sec + 1) % 4, f, other)))
    for other in range(4):
        rdma(lsend.at[other], lrecv.at[other], ls.at[other], lr.at[other], ((sec + 1) % 4, f, other)).wait_recv()

    pieces = [lrecv[other].astype(jnp.float32) for other in range(4)]
    tiles = []
    for other in range(4):
        first = pieces[other][:, :128]
        if other:
            first = first + pieces[other - 1][:, 512:]
        tiles.append(first)
        tiles.append(pieces[other][:, 128:512])
    latent = jnp.concatenate(tiles, axis=1)
    rope = pieces[3][:, 512:]

    q = latent[:, :QL]
    q_out[...] = (
        q * lax.rsqrt(jnp.mean(q * q, axis=1, keepdims=True) + epsilon) * q_gain_v[...][None, :]
    ).astype(jnp.bfloat16)
    k = latent[:, QL:]
    kv_out[:, :KVL] = (
        k * lax.rsqrt(jnp.mean(k * k, axis=1, keepdims=True) + epsilon) * kv_gain_v[...][None, :]
    ).astype(jnp.bfloat16)
    lane = lax.broadcasted_iota(jnp.int32, rope.shape, 1)
    swapped = jnp.where(lane < ROPE // 2, pltpu.roll(rope, 128 - ROPE // 2, 1), pltpu.roll(rope, ROPE // 2, 1))
    turned = rope * cosine[...] + swapped * sine[...]
    kv_out[:, KVL:] = turned[:, :ROPE].astype(jnp.bfloat16)

    for copy in sends:
        copy.wait_send()
    def sent(i, carry):
        rows = w_rows(0, 0)
        rdma(rows, rows, zs.at[i], zr.at[i], ahead_z).wait_send()
        rdma(rows, rows, ys.at[PARTS + i], yr.at[PARTS + i], ahead_y).wait_send()
        return carry

    lax.fori_loop(0, HOPS * PARTS, sent, 0)
    for d in range(1, HOPS):
        cross(0, HOPS - 1 + d).wait_send()

    @pl.when(core == 1)
    def _():
        for part in range(PARTS):
            rows = w_rows(0, 0)
            rdma(rows, rows, ys.at[part], yr.at[part], ahead_y).wait_send()
        cross(0, HOPS - 1).wait_send()


def on_device(hidden, attn_gain, q_gain, kv_gain, down_weight):
    quarter = QUARTER
    vmem = pl.BlockSpec(memory_space=pltpu.VMEM)
    free = pl.BlockSpec(memory_space=pl.ANY)
    hbm = pl.BlockSpec(memory_space=pltpu.HBM)
    dma = pltpu.SemaphoreType.DMA
    return pl.pallas_call(
        kernel,
        out_shape=(
            jax.ShapeDtypeStruct((quarter, QL), jnp.bfloat16),
            jax.ShapeDtypeStruct((quarter, KVL + ROPE), jnp.bfloat16),
        ),
        in_specs=[hbm, free, hbm, hbm, hbm],
        out_specs=(vmem, vmem),
        scratch_shapes=[
            pltpu.VMEM((4, ROWS, KS), jnp.bfloat16),
            pltpu.VMEM((4, ROWS, KS), jnp.bfloat16),
            pltpu.VMEM((D, WC), jnp.bfloat16),
            pltpu.VMEM((ROWS, WIDE), jnp.float32),
            pltpu.VMEM((ROWS, 128), jnp.float32),
            pltpu.VMEM((4, QUARTER, WIDE), jnp.bfloat16),
            pltpu.VMEM((4, QUARTER, WIDE), jnp.bfloat16),
            pltpu.VMEM((D,), jnp.float32),
            pltpu.VMEM((QL,), jnp.float32),
            pltpu.VMEM((KVL,), jnp.float32),
            pltpu.VMEM((QUARTER, 128), jnp.float32),
            pltpu.VMEM((QUARTER, 128), jnp.float32),
            dma((5,)),
            dma((6,)), dma((6,)),
            dma((HOPS * PARTS,)), dma((HOPS * PARTS,)),
            dma(((HOPS + 1) * PARTS,)), dma(((HOPS + 1) * PARTS,)),
            dma((2 * HOPS - 1,)), dma((2 * HOPS - 1,)),
            dma((4,)), dma((4,)),
            pltpu.SemaphoreType.REGULAR((4,)),
        ],
        compiler_params=pltpu.CompilerParams(collective_id=0, has_side_effects=True, vmem_limit_bytes=56_000_000),
    )(
        hidden, down_weight, attn_gain, q_gain, kv_gain,
    )


def solution(mesh):
    placed = (P(("section", "fsdp"), "ep"), P(), P(), P(), P("fsdp", "ep"))
    return jax.shard_map(
        on_device,
        mesh=mesh,
        in_specs=placed,
        out_specs=(P(("section", "fsdp", "ep"), None), P(("section", "fsdp", "ep"), None)),
        check_vma=False,
    )
```

```python
import functools

import jax
import jax.numpy as jnp
from jax import lax
from jax.experimental import pallas as pl
from jax.experimental.pallas import tpu as pltpu
from jax.sharding import PartitionSpec as P

MESH = pl.DeviceIdType.MESH

QL = 1536
KVL = 512
ROPE = 64
LENGTH = 4096
D = 7168

epsilon = 1e-06
rope_base = 10000.0

ROWS = 256
KS = 1792
WR = 224
WC = 528
PARTS = 7
PR = WR // PARTS
GROUP = 4 * WR
HALF = ROWS // 2
QUARTER = ROWS // 4
WIDE = 640
NZ = 16
HOPS = NZ // 2


def kernel(
    hid, w, gain, q_gain, kv_gain, q_out, kv_out,
    xbuf, xg, wbuf, acc, ssq, lsend, lrecv, gain_v, q_gain_v, kv_gain_v, cosine, sine,
    local_sem, xs, xr, zs, zr, ys, yr, cs, cr, ls, lr, rounds,
):
    sec = lax.axis_index("section")
    f = lax.axis_index("fsdp")
    x = lax.axis_index("ep")
    core = sec % 2
    yl = f // NZ
    z = f % NZ
    y = (sec // 2) * 2 + yl
    way = 1 - 2 * core

    def place(y_, z_, core_, x_):
        y_ = (y_ + 8) % 4
        z_ = (z_ + 2 * NZ) % NZ
        return ((y_ // 2) * 2 + core_, (y_ % 2) * NZ + z_, (x_ + 4) % 4)

    ahead_z = place(y, z + way, core, x)
    ahead_y = place(y + way, z, core, x)
    sibling = place(y, z, 1 - core, x)
    right = place(y, z, core, x + 1)
    left = place(y, z, core, x - 1)

    barrier = pltpu.get_barrier_semaphore()
    up_y, down_y = place(y + 1, z, core, x), place(y - 1, z, core, x)
    partners = [place(y, z + 1, core, x), place(y, z - 1, core, x), up_y, down_y, sibling, right, left]

    def tell(semaphore, devices):
        for device in devices:
            pl.semaphore_signal(semaphore, inc=1, device_id=device, device_id_type=MESH)

    tell(barrier, partners)
    pl.semaphore_wait(barrier, len(partners))

    tell(rounds.at[0], (right, left))

    def next_round(n):
        if n < 3:
            pl.semaphore_wait(rounds.at[n], 2)
            tell(rounds.at[n + 1], (up_y, down_y) if n < 2 else (sibling,))
        else:
            pl.semaphore_wait(rounds.at[n], 1)

    def rdma(src, dst, send, recv, device):
        return pltpu.make_async_remote_copy(
            src_ref=src, dst_ref=dst, send_sem=send, recv_sem=recv,
            device_id=device, device_id_type=MESH,
        )

    sends = []

    def start(copy):
        copy.start()
        sends.append(copy)

    def x_rows(owner, half):
        return xbuf.at[owner, pl.ds(half * HALF, HALF)]

    def x_own(half, index, device):
        return rdma(hid.at[pl.ds(half * HALF, HALF)], x_rows(x, half), xs.at[index], xr.at[index], device)

    x_left, x_right, x_far = (x + 3) % 4, (x + 1) % 4, (x + 2) % 4

    def w_rows(slot, part):
        return wbuf.at[pl.ds(pl.multiple_of(slot * WR + part * PR, PR), PR)]

    def ring_slot(d):
        return yl * NZ + (z - way * d + NZ) % NZ

    def pair_slot(d):
        return (1 - yl) * NZ + (z - way * d + NZ) % NZ

    def w_src(d, part):
        if d == 0:
            return w.at[pl.ds(part * PR, PR)]
        return w_rows(ring_slot(d), part)

    own_x = pltpu.make_async_copy(hid, xbuf.at[x], local_sem.at[0])
    own_gains = [
        pltpu.make_async_copy(gain, gain_v, local_sem.at[2]),
        pltpu.make_async_copy(q_gain, q_gain_v, local_sem.at[3]),
        pltpu.make_async_copy(kv_gain, kv_gain_v, local_sem.at[4]),
    ]
    own_w = pltpu.make_async_copy(w, wbuf.at[pl.ds(pl.multiple_of(f * WR, WR), WR)], local_sem.at[1])

    def z_copy(d, part):
        i = d * PARTS + part
        return rdma(w_src(d, part), w_rows(ring_slot(d), part), zs.at[i], zr.at[i], ahead_z)

    def y_copy(d, part):
        i = d * PARTS + part
        return rdma(w_src(d, part), w_rows(ring_slot(d), part), ys.at[i], yr.at[i], ahead_y)

    def shard(slot):
        return wbuf.at[pl.ds(pl.multiple_of(slot * WR, WR), WR)]

    def cross(slot, i):
        return rdma(shard(slot), shard(slot), cs.at[i], cr.at[i], sibling)

    def each_part(step):
        def body(part, carry):
            step(part)
            return carry

        lax.fori_loop(0, PARTS, body, 0)

    def await_pair(d):
        def step(part):
            i = d * PARTS + part
            rows = w_rows(0, 0)
            rdma(rows, rows, ys.at[i], yr.at[i], ahead_y).wait_recv()

        each_part(step)

    def hand_on_pair(d):
        await_pair(d)
        cross(pair_slot(d), HOPS - 1 + d).start()

    def angles():
        half_rope = ROPE // 2
        shape = (QUARTER, 128)
        lane = lax.broadcasted_iota(jnp.int32, shape, 1)
        row = lax.broadcasted_iota(jnp.int32, shape, 0) + f * ROWS + x * QUARTER
        power = (lane % half_rope).astype(jnp.float32) / half_rope
        angle = (row % LENGTH).astype(jnp.float32) * (rope_base ** (-power))
        cosine[...] = jnp.cos(angle)
        sine[...] = jnp.where(lane < half_rope, -jnp.sin(angle), jnp.sin(angle))

    def prepare(owner, half):
        g = gain_v[pl.ds(pl.multiple_of(owner * KS, KS), KS)][None, :]

        def block(i, carry):
            rows = pl.ds(pl.multiple_of(half * HALF + i * 16, 16), 16)
            v = xbuf[owner, rows, :].astype(jnp.float32)
            xg[owner, rows, :] = (v * g).astype(jnp.bfloat16)
            total = ssq[rows, :]
            for t in range(KS // 128):
                piece = v[:, t * 128 : (t + 1) * 128]
                total = total + piece * piece
            ssq[rows, :] = total
            return carry

        lax.fori_loop(0, HALF // 16, block, 0)

    def multiply(parity, z_from):
        group = parity * (NZ // 4) + z_from % NZ // 4
        owner = group // 2
        depth = pl.ds(pl.multiple_of(group % 2 * GROUP, GROUP), GROUP)
        columns = wbuf[pl.ds(pl.multiple_of(group * GROUP, GROUP), GROUP), :]
        acc[:, :WC] += jnp.dot(xg[owner, :, depth], columns, preferred_element_type=jnp.float32)

    def near_owner(parity):
        return (parity * (NZ // 4) + z // 4) // 2

    def multiply_all(parity, first_step, last_step):
        def body(i, carry):
            multiply(parity, z + 4 * i)
            return carry

        lax.fori_loop(first_step, last_step + 1, body, 0)

    def await_cross(first_index, last_index):
        for i in range(first_index, last_index + 1):
            cross(0, i).wait_recv()

    def first(part):
        z_copy(0, part).start()

        @pl.when(core == 1)
        def _():
            y_copy(0, part).start()

    each_part(first)
    start(x_own(0, 0, right))
    start(x_own(1, 1, left))
    start(x_own(1, 2, right))
    start(x_own(0, 3, left))
    own_x.start()
    own_w.start()
    for copy in own_gains:
        copy.start()
    angles()
    ssq[...] = jnp.zeros_like(ssq)
    acc[...] = jnp.zeros_like(acc)
    own_x.wait()
    for copy in own_gains:
        copy.wait()
    prepare(x, 0)
    prepare(x, 1)
    own_w.wait()

    for d in range(1, HOPS + 1):

        def step(part):
            z_copy(d - 1, part).wait_recv()
            if d < HOPS:
                z_copy(d, part).start()
            y_copy(d, part).start()

        each_part(step)
        if d < HOPS:
            start(cross(ring_slot(d), d - 1))
        if d == 2:

            @pl.when(core == 1)
            def _():
                hand_on_pair(0)

        if d >= 3:
            hand_on_pair(d - 2)
        if d <= 4:
            next_round(d - 1)
        if d == 5:
            x_own(0, 0, right).wait_recv()
            start(rdma(x_rows(x_left, 0), x_rows(x_left, 0), xs.at[4], xr.at[4], right))
            x_own(1, 1, left).wait_recv()
            start(rdma(x_rows(x_right, 1), x_rows(x_right, 1), xs.at[5], xr.at[5], left))
        if d == 6:
            prepare(x_left, 0)
            prepare(x_right, 1)
        if d == 7:
            x_own(1, 2, right).wait_recv()
            prepare(x_left, 1)
            x_own(0, 3, left).wait_recv()
            prepare(x_right, 0)
            await_cross(0, 2)

            @pl.when(near_owner(yl) != x_far)
            def _():
                multiply(yl, z)

            @pl.when(core == 0)
            def _():
                await_cross(HOPS - 1, HOPS - 1)

            await_cross(HOPS, HOPS + 2)

            @pl.when(near_owner(1 - yl) != x_far)
            def _():
                multiply(1 - yl, z)

    hand_on_pair(HOPS - 1)
    for half in range(2):
        rows = x_rows(x_far, half)
        rdma(rows, rows, xs.at[4 + half], xr.at[4 + half], right).wait_recv()
        prepare(x_far, half)
    @pl.when(near_owner(yl) == x_far)
    def _():
        multiply(yl, z)

    @pl.when(near_owner(1 - yl) == x_far)
    def _():
        multiply(1 - yl, z)

    await_cross(3, HOPS - 2)
    multiply_all(yl, 1, 3)

    await_cross(HOPS + 3, 2 * HOPS - 2)
    multiply_all(1 - yl, 3, 3)
    multiply_all(1 - yl, 5, 5)
    await_pair(HOPS)
    multiply_all(1 - yl, 6, 6)

    scale = lax.rsqrt(jnp.sum(ssq[...], axis=1, keepdims=True) / D + epsilon)
    out = pltpu.roll(acc[...] * scale, x * 16, 1).astype(jnp.bfloat16)
    for other in range(4):
        lsend[other] = out[other * QUARTER : (other + 1) * QUARTER]
    for other in range(4):
        start(rdma(lsend.at[other], lrecv.at[x], ls.at[other], lr.at[x], ((sec + 1) % 4, f, other)))
    for other in range(4):
        rdma(lsend.at[other], lrecv.at[other], ls.at[other], lr.at[other], ((sec + 1) % 4, f, other)).wait_recv()

    pieces = [lrecv[other].astype(jnp.float32) for other in range(4)]
    tiles = []
    for other in range(4):
        first = pieces[other][:, :128]
        if other:
            first = first + pieces[other - 1][:, 512:]
        tiles.append(first)
        tiles.append(pieces[other][:, 128:512])
    latent = jnp.concatenate(tiles, axis=1)
    rope = pieces[3][:, 512:]

    q = latent[:, :QL]
    q_out[...] = (
        q * lax.rsqrt(jnp.mean(q * q, axis=1, keepdims=True) + epsilon) * q_gain_v[...][None, :]
    ).astype(jnp.bfloat16)
    k = latent[:, QL:]
    kv_out[:, :KVL] = (
        k * lax.rsqrt(jnp.mean(k * k, axis=1, keepdims=True) + epsilon) * kv_gain_v[...][None, :]
    ).astype(jnp.bfloat16)
    lane = lax.broadcasted_iota(jnp.int32, rope.shape, 1)
    swapped = jnp.where(lane < ROPE // 2, pltpu.roll(rope, 128 - ROPE // 2, 1), pltpu.roll(rope, ROPE // 2, 1))
    turned = rope * cosine[...] + swapped * sine[...]
    kv_out[:, KVL:] = turned[:, :ROPE].astype(jnp.bfloat16)

    for copy in sends:
        copy.wait_send()
    def sent(i, carry):
        rows = w_rows(0, 0)
        rdma(rows, rows, zs.at[i], zr.at[i], ahead_z).wait_send()
        rdma(rows, rows, ys.at[PARTS + i], yr.at[PARTS + i], ahead_y).wait_send()
        return carry

    lax.fori_loop(0, HOPS * PARTS, sent, 0)
    for d in range(1, HOPS):
        cross(0, HOPS - 1 + d).wait_send()

    @pl.when(core == 1)
    def _():
        for part in range(PARTS):
            rows = w_rows(0, 0)
            rdma(rows, rows, ys.at[part], yr.at[part], ahead_y).wait_send()
        cross(0, HOPS - 1).wait_send()


def on_device(hidden, attn_gain, q_gain, kv_gain, down_weight):
    quarter = QUARTER
    vmem = pl.BlockSpec(memory_space=pltpu.VMEM)
    free = pl.BlockSpec(memory_space=pl.ANY)
    hbm = pl.BlockSpec(memory_space=pltpu.HBM)
    dma = pltpu.SemaphoreType.DMA
    return pl.pallas_call(
        kernel,
        out_shape=(
            jax.ShapeDtypeStruct((quarter, QL), jnp.bfloat16),
            jax.ShapeDtypeStruct((quarter, KVL + ROPE), jnp.bfloat16),
        ),
        in_specs=[hbm, free, hbm, hbm, hbm],
        out_specs=(vmem, vmem),
        scratch_shapes=[
            pltpu.VMEM((4, ROWS, KS), jnp.bfloat16),
            pltpu.VMEM((4, ROWS, KS), jnp.bfloat16),
            pltpu.VMEM((D, WC), jnp.bfloat16),
            pltpu.VMEM((ROWS, WIDE), jnp.float32),
            pltpu.VMEM((ROWS, 128), jnp.float32),
            pltpu.VMEM((4, QUARTER, WIDE), jnp.bfloat16),
            pltpu.VMEM((4, QUARTER, WIDE), jnp.bfloat16),
            pltpu.VMEM((D,), jnp.float32),
            pltpu.VMEM((QL,), jnp.float32),
            pltpu.VMEM((KVL,), jnp.float32),
            pltpu.VMEM((QUARTER, 128), jnp.float32),
            pltpu.VMEM((QUARTER, 128), jnp.float32),
            dma((5,)),
            dma((6,)), dma((6,)),
            dma((HOPS * PARTS,)), dma((HOPS * PARTS,)),
            dma(((HOPS + 1) * PARTS,)), dma(((HOPS + 1) * PARTS,)),
            dma((2 * HOPS - 1,)), dma((2 * HOPS - 1,)),
            dma((4,)), dma((4,)),
            pltpu.SemaphoreType.REGULAR((4,)),
        ],
        compiler_params=pltpu.CompilerParams(collective_id=0, has_side_effects=True, vmem_limit_bytes=56_000_000),
    )(
        hidden, down_weight, attn_gain, q_gain, kv_gain,
    )


def solution(mesh):
    placed = (P(("section", "fsdp"), "ep"), P(), P(), P(), P("fsdp", "ep"))
    return jax.shard_map(
        on_device,
        mesh=mesh,
        in_specs=placed,
        out_specs=(P(("section", "fsdp", "ep"), None), P(("section", "fsdp", "ep"), None)),
        check_vma=False,
    )
```
